32 devices in a mesh: blk: 8 (over y, x, core), grp: 4 (over z).
Axes of the slice: x: 2, y: 2, z: 4, core: 2. Of those that a mesh axis runs over, the one named last changes fastest.
Arguments:
- blocks: bfloat16 [64, 12, 128, 128], P(('blk', 'grp')), may hold values from -0.5 to 0.5
- neighbours: int32 [64, 12], P(('blk', 'grp')), may hold values from 0 to 9
- tentative: bfloat16 [64, 128, 128], P(('blk', 'grp')), may hold values from -0.5 to 0.5
- inv_diag: float32 [64, 128], P(('blk', 'grp')), may hold values from 0.5 to 2
- coarse_map: int32 [8, 4, 2], P(None, 'grp'), may hold values from 0 to 1
- counts: int32 [32], P(('blk', 'grp')), may hold values from 1 to 2, as said below
Outputs:
- coarse: float32 [16, 5, 2, 128, 128], P('blk', None, None, 'grp')
The draws below stay inside these ranges and needn't reach their ends.
Inputs may be any that keep to these rules, and one draw needn't show every extreme that they name: `counts`: each device's set holds 1 or 2 live rows; at least one device holds 2.
All inputs are finite; a program needn't handle non-finite values.
Results may differ from the reference program's by a relative error of at most 0.0034.
Values may be sent and summed in bfloat16 or wider, within the bound.
No kernel may reach another device: no remote copies, remote signals or barrier semaphores. Data moves between devices by JAX's collectives and lax.ppermute only.
A program may use at most 64 MiB of HBM per device.

```python
import math
import jax
import jax.numpy as jnp
from jax import lax

PORES = 128
COARSE_W = 128
NNZ = 12
NB_DEV = 2
NCG = 2
NBLOCKS = 64
DEVSET = 32
N_BLK = 8
N_GRP = 4


def draw_counts(key, part):
    first, second = jax.random.split(jax.random.fold_in(key, 7))
    values = jax.random.randint(first, (DEVSET,), max(1, NB_DEV // 4), NB_DEV + 1)
    chosen = jax.random.randint(second, (), 0, DEVSET)
    return jnp.where(jnp.arange(DEVSET) == chosen, NB_DEV, values).astype(jnp.int32)


def set_ends(values, rng, smallest, top_value):
    dims = values.shape
    index_at = [jax.random.randint(jax.random.fold_in(rng, axis), (), 0, dims[axis]) for axis in range(len(dims))]
    values = values.at[tuple(index_at)].set(smallest)
    longest = dims.index(max(dims))
    index_at[longest] = (index_at[longest] + 1) % dims[longest]
    return values.at[tuple(index_at)].set(top_value)


def block_levels(stream_key, shape, cuts, least, high):
    gain = 1.0
    for position, parts in cuts:
        heights = jax.random.uniform(jax.random.fold_in(jax.random.fold_in(stream_key, 6), position), (parts,), jnp.float32, least / len(cuts), high / len(cuts))
        gain = gain * jnp.repeat(jnp.exp(heights), shape[position] // parts).reshape((-1,) + (1,) * (len(shape) - 1 - position))
    return gain


def bell_draw(key, shape, spread, bound, shards=(), held_as=jnp.bfloat16):
    values = spread * jax.random.normal(key, shape, jnp.float32)
    if shards:
        values = values * block_levels(key, shape, shards, -0.22, 0.18)
    return jnp.clip(values, -bound, bound).astype(held_as)


def setup_inputs(seed: int = 0) -> dict:
    splits = jax.random.split(jax.random.key(seed), 7)
    return {
        "blocks": bell_draw(splits[0], (NBLOCKS, NNZ, PORES, PORES), PORES ** -0.5, 0.5, ((0, 32),)),
        "neighbours": set_ends(jax.random.randint(splits[1], (NBLOCKS, NNZ), 0, 5 * NB_DEV), jax.random.fold_in(splits[1], 1), 0, (5 * NB_DEV) - 1).astype(jnp.int32),
        "tentative": bell_draw(splits[2], (NBLOCKS, PORES, COARSE_W), PORES ** -0.5, 0.5, ((0, 32),)),
        "inv_diag": jnp.clip(jnp.exp(math.log(2.0) - 1.3862944 * jax.random.uniform(splits[3], (NBLOCKS, PORES), jnp.float32) ** block_levels(splits[3], (NBLOCKS, PORES), ((0, 32),), -0.2, 0.2)), 0.5, 2.0),
        "coarse_map": set_ends(jax.random.randint(splits[4], (N_BLK, N_GRP, NB_DEV), 0, NCG), jax.random.fold_in(splits[4], 1), 0, NCG - 1).astype(jnp.int32),
        "counts": draw_counts(jax.random.fold_in(splits[6], 71), 0),
    }


omega = 0.6


def reference(blocks, neighbours, tentative, inv_diag, coarse_map, counts):
    live = (jnp.arange(NB_DEV, dtype=jnp.int32)[None, :] < counts[:, None]).reshape(N_BLK, N_GRP, NB_DEV, 1, 1)
    blocks6 = blocks.reshape(N_BLK, N_GRP, NB_DEV, NNZ, PORES, PORES)
    neigh3 = neighbours.reshape(N_BLK, N_GRP, NB_DEV, NNZ)
    tent = tentative.reshape(N_BLK, N_GRP, NB_DEV, PORES, COARSE_W)
    masked = jnp.where(live, tent, jnp.zeros_like(tent))
    scale = inv_diag.reshape(N_BLK, N_GRP, NB_DEV, PORES, 1)

    def neighbour_maps(b):
        window = jnp.concatenate([coarse_map[(b + offset) % N_BLK] for offset in (-2, -1, 0, 1, 2)], axis=1)
        found = jnp.take_along_axis(window, neigh3[b].reshape(N_GRP, NB_DEV * NNZ), axis=1)
        return found.reshape(N_GRP, NB_DEV, NNZ)

    def smooth_group(b):
        same_block = (neigh3[b] // NB_DEV == 2) & (neighbour_maps(b) == coarse_map[b][:, :, None])
        picked = jax.vmap(lambda panel_pool, index: panel_pool[index])(masked[b], neigh3[b] % NB_DEV)
        picked = jnp.where(same_block[..., None, None], picked, jnp.zeros_like(picked))
        return jnp.einsum('gsnij,gsnjk->gsik', blocks6[b].astype(jnp.float32), picked.astype(jnp.float32))

    smoothing = lax.map(smooth_group, jnp.arange(N_BLK, dtype=jnp.int32))
    prolong = jnp.where(live, tent.astype(jnp.float32) - omega * scale * smoothing, jnp.float32(0.0)).astype(jnp.bfloat16)
    targets = jnp.arange(NCG * 5 * NCG, dtype=jnp.int32)

    def coarse_group(b):
        pieces = jnp.concatenate([prolong[(b + offset) % N_BLK] for offset in (-2, -1, 0, 1, 2)], axis=1)
        picked = jax.vmap(lambda panel_pool, index: panel_pool[index])(pieces, neigh3[b])
        pair = jnp.einsum('gsnij,gsnjk->gsnik', blocks6[b].astype(jnp.float32), picked.astype(jnp.float32)).astype(jnp.bfloat16)
        galerkin = jnp.einsum('gsik,gsnij->gsnkj', prolong[b].astype(jnp.float32), pair.astype(jnp.float32))
        dest_index = (coarse_map[b][:, :, None] * 5 + neigh3[b] // NB_DEV) * NCG + neighbour_maps(b)
        onehot = (dest_index.reshape(-1)[None, :] == targets[:, None]).astype(jnp.float32)
        summed = jnp.dot(onehot, galerkin.reshape(N_GRP * NB_DEV * NNZ, COARSE_W * COARSE_W), precision=lax.Precision.HIGHEST)
        return summed.reshape(NCG, 5, NCG, COARSE_W, COARSE_W)

    coarse = lax.map(coarse_group, jnp.arange(N_BLK, dtype=jnp.int32))
    return coarse.reshape(N_BLK * NCG, 5, NCG, COARSE_W, COARSE_W)
```

```python
import functools

import jax
import jax.numpy as jnp
from jax import lax
from jax.experimental import pallas as pl
from jax.experimental.pallas import tpu as pltpu
from jax.sharding import PartitionSpec as P

NCG = 2
OFFSETS = 5
GROUP = 8
omega = 0.6

SMEM = pl.BlockSpec(memory_space=pltpu.SMEM)
VMEM = pl.BlockSpec(memory_space=pltpu.VMEM)


def from_behind(block, axis, distance):
    size = lax.axis_size(axis)
    return lax.ppermute(block, axis, [((i - distance) % size, i) for i in range(size)])


def from_sibling(block):
    size = lax.axis_size("blk")
    return lax.ppermute(block, "blk", [(i ^ 1, i) for i in range(size)])


def prolong_kernel(ids, neighbours, coarse_map, counts, blocks, tentative, inv_diag, out, pool):
    slots, nnz = neighbours.shape
    here = ids[0]
    live = counts[0]
    for slot in range(slots):
        pool[slot] = tentative[slot]
    pool[slots] = jnp.zeros_like(pool[slots])
    for row in range(slots):
        mine = coarse_map[here, 0, row]
        total = None
        for n in range(nnz):
            code = neighbours[row, n]
            slot = code - 2 * slots
            inside = (slot >= 0) & (slot < live)
            kept = inside & (coarse_map[here, 0, jnp.clip(slot, 0, slots - 1)] == mine)
            term = jnp.dot(
                blocks[row, n],
                pool[jnp.where(kept, slot, slots)],
                preferred_element_type=jnp.float32,
            )
            total = term if total is None else total + term
        width = out.shape[2]
        scale = jnp.broadcast_to(omega * inv_diag[row : row + 1, :], (width, inv_diag.shape[1])).T
        value = tentative[row].astype(jnp.float32) - scale * total
        out[row] = jnp.where(row < live, value, 0.0).astype(out.dtype)


def prolong_call(ids, neighbours, coarse_map, counts, blocks, tentative, inv_diag):
    slots, pores, width = tentative.shape
    return pl.pallas_call(
        prolong_kernel,
        out_shape=jax.ShapeDtypeStruct(tentative.shape, tentative.dtype),
        in_specs=[SMEM, SMEM, SMEM, SMEM, VMEM, VMEM, VMEM],
        out_specs=VMEM,
        scratch_shapes=[pltpu.VMEM((slots + 1, pores, width), tentative.dtype)],
        compiler_params=pltpu.CompilerParams(vmem_limit_bytes=16 << 20),
        cost_estimate=pl.CostEstimate(flops=100_000_000, bytes_accessed=1_000_000, transcendentals=0),
        name="prolong",
    )(ids, neighbours, coarse_map, counts, blocks, tentative, inv_diag)


def galerkin_kernel(places, parts, ids, neighbours, coarse_map, blocks, own, *refs):
    panels = len({p for parity in places for p in parity if p >= 0})
    extra = panels - (1 if 0 in places[0] and places[0][2] == 0 else 0)
    halo = refs[:extra]
    outs = refs[extra : extra + parts]
    pool, flipped, acc, todo = refs[extra + parts :]
    slots, nnz = neighbours.shape
    here, group = ids[0], ids[1]
    cycle = coarse_map.shape[0]
    odd = lax.rem(here, 2)

    first = panels - extra
    if first:
        for slot in range(slots):
            pool[slot] = own[slot]
    for i, panel in enumerate(halo):
        for slot in range(slots):
            pool[(first + i) * slots + slot] = panel[slot]
    for row in range(slots):
        flipped[row] = own[row].T
    dests = NCG * panels * NCG
    acc[...] = jnp.zeros_like(acc)

    for i in range(slots * nnz + GROUP):
        todo[i] = 0
        todo[i + slots * nnz + GROUP] = 0
        todo[i + 2 * (slots * nnz + GROUP)] = dests
    stride = slots * nnz + GROUP
    count = jnp.int32(0)
    for row in range(slots):
        mine = coarse_map[here, 0, row]
        for n in range(nnz):
            code = neighbours[row, n]
            offset = lax.div(code, slots)
            slot = code - offset * slots
            place = jnp.int32(-1)
            for o in range(OFFSETS):
                place = jnp.where(offset == o, jnp.where(odd == 1, places[1][o], places[0][o]), place)
            other = coarse_map[lax.rem(here + offset - 2 + cycle, cycle), 0, slot]
            wanted = place >= 0
            at = count
            todo[at] = row * nnz + n
            todo[at + stride] = jnp.where(wanted, place * slots + slot, 0)
            todo[at + 2 * stride] = jnp.where(wanted, (mine * panels + place) * NCG + other, dests)
            count = count + wanted.astype(jnp.int32)

    def some(step, carry):
        grams = []
        for j in range(GROUP):
            at = step * GROUP + j
            entry = todo[at]
            pair = jnp.dot(
                blocks[entry], pool[todo[at + stride]], preferred_element_type=jnp.float32
            ).astype(own.dtype)
            row = lax.div(entry, nnz)
            grams.append(jnp.dot(flipped[row], pair, preferred_element_type=jnp.float32))
        for j in range(GROUP):
            dest = todo[step * GROUP + j + 2 * stride]
            acc[dest] = acc[dest] + grams[j]
        return carry

    lax.fori_loop(0, lax.div(count + GROUP - 1, GROUP), some, 0)

    rows = outs[0].shape[1]
    for distance in range(parts):
        target = lax.rem(group + distance, parts)
        start = pl.multiple_of(target * rows, rows)
        for dest in range(dests):
            outs[distance][dest] = acc[dest, pl.ds(start, rows), :].astype(outs[distance].dtype)


def galerkin_call(places, parts, ids, neighbours, coarse_map, blocks, own, halo, name):
    slots, pores, width = own.shape
    nnz = neighbours.shape[1]
    panels = len({p for parity in places for p in parity if p >= 0})
    dests = NCG * panels * NCG
    rows = width // parts
    outs = [jax.ShapeDtypeStruct((dests, rows, width), jnp.float32 if d == 0 else own.dtype) for d in range(parts)]
    return pl.pallas_call(
        functools.partial(galerkin_kernel, places, parts),
        out_shape=outs,
        in_specs=[SMEM, SMEM, SMEM, VMEM, VMEM] + [VMEM] * len(halo),
        out_specs=[VMEM] * parts,
        scratch_shapes=[
            pltpu.VMEM((panels * slots, pores, width), own.dtype),
            pltpu.VMEM((slots, width, pores), own.dtype),
            pltpu.VMEM((dests + 1, width, width), jnp.float32),
            pltpu.SMEM((3 * (slots * nnz + GROUP),), jnp.int32),
        ],
        compiler_params=pltpu.CompilerParams(vmem_limit_bytes=24 << 20),
        cost_estimate=pl.CostEstimate(flops=200_000_000, bytes_accessed=2_000_000, transcendentals=0),
        name=name,
    )(ids, neighbours, coarse_map, blocks.reshape(slots * nnz, pores, pores), own, *halo)


NEAR = ((-1, -1, 0, 1, -1), (-1, 1, 0, -1, -1))
FAR = ((0, 2, -1, -1, 1), (0, -1, -1, 2, 1))


def finish_kernel(parts, ids, *refs):
    near, far, out = refs[:parts], refs[parts : 2 * parts], refs[2 * parts]
    odd = lax.rem(ids[0], 2) == 1
    for places, pieces in ((NEAR, near), (FAR, far)):
        panels = max(places[0]) + 1
        for c in range(NCG):
            for panel in range(panels):
                offset = jnp.where(odd, places[1].index(panel), places[0].index(panel))
                for c2 in range(NCG):
                    dest = (c * panels + panel) * NCG + c2
                    total = pieces[0][dest].astype(jnp.float32)
                    for piece in pieces[1:]:
                        total = total + piece[dest].astype(jnp.float32)
                    out[c, offset, c2] = total


def finish_call(ids, near, far, rows, width):
    parts = len(near)
    return pl.pallas_call(
        functools.partial(finish_kernel, parts),
        out_shape=jax.ShapeDtypeStruct((NCG, OFFSETS, NCG, rows, width), jnp.float32),
        in_specs=[SMEM] + [VMEM] * (2 * parts),
        out_specs=VMEM,
        compiler_params=pltpu.CompilerParams(vmem_limit_bytes=16 << 20),
        cost_estimate=pl.CostEstimate(flops=1_000_000, bytes_accessed=1_500_000, transcendentals=0),
        name="finish",
    )(ids, *near, *far)


def spread(pieces):
    parts = lax.axis_size("grp")
    rows = pieces[0].shape[1]
    return [pieces[0]] + [from_behind(pieces[d], "grp", d) for d in range(1, parts)]


def local(blocks, neighbours, tentative, inv_diag, coarse_map, counts):
    parts = lax.axis_size("grp")
    slots, pores, width = tentative.shape
    ids = jnp.stack([lax.axis_index("blk"), lax.axis_index("grp")]).astype(jnp.int32)
    own = prolong_call(ids, neighbours, coarse_map, counts, blocks, tentative, inv_diag)
    sibling = from_sibling(own)
    behind = from_behind(own, "blk", 2)
    ahead = from_behind(own, "blk", -2)
    odd = lax.rem(lax.axis_index("blk"), 2) == 1
    split = parts <= 4
    share = parts if split else 1
    near = galerkin_call(NEAR, share, ids, neighbours, coarse_map, blocks, own, [sibling], "near")
    if split:
        near = spread(near)
    other = from_sibling(jnp.where(odd, behind, ahead))
    far = galerkin_call(FAR, share, ids, neighbours, coarse_map, blocks, own, [behind, ahead, other], "far")
    if split:
        far = spread(far)
    else:
        near, far = [gathered(near[0], parts)], [gathered(far[0], parts)]
    return finish_call(ids, near, far, width // parts, width)


def gathered(whole, parts):
    dests, width, _ = whole.shape
    pieces = whole.astype(jnp.bfloat16).reshape(dests, parts, width // parts, width)
    arrived = lax.all_to_all(pieces, "grp", 1, 1, tiled=True)
    return jnp.sum(arrived.astype(jnp.float32), axis=1)


def solution(mesh):
    return jax.shard_map(
        local,
        mesh=mesh,
        in_specs=(
            P(("blk", "grp"), None, None, None),
            P(("blk", "grp"), None),
            P(("blk", "grp"), None, None),
            P(("blk", "grp"), None),
            P(None, "grp", None),
            P(("blk", "grp")),
        ),
        out_specs=P("blk", None, None, "grp", None),
        check_vma=False,
    )
```

```python
import functools

import jax
import jax.numpy as jnp
from jax import lax
from jax.experimental import pallas as pl
from jax.experimental.pallas import tpu as pltpu
from jax.sharding import PartitionSpec as P

NCG = 2
OFFSETS = 5
NEAR = 2
FAR = 3
omega = 0.6

SMEM = pl.BlockSpec(memory_space=pltpu.SMEM)
VMEM = pl.BlockSpec(memory_space=pltpu.VMEM)
ANY = pl.BlockSpec(memory_space=pltpu.HBM)


def from_behind(block, axis, distance):
    size = lax.axis_size(axis)
    return lax.ppermute(block, axis, [((i - distance) % size, i) for i in range(size)])


def from_sibling(block):
    size = lax.axis_size("blk")
    return lax.ppermute(block, "blk", [(i ^ 1, i) for i in range(size)])


def from_across(block):
    size = lax.axis_size("blk")
    return lax.ppermute(block, "blk", [((i + (1 if i % 2 else -1)) % size, i) for i in range(size)])


def prolong_kernel(counts, neighbours, coarse_map, blocks, tentative, inv_diag, out, flipped, todo,
                   held, base, scale, codes, groups, table, sems):
    slots, nnz = neighbours.shape
    cycle = coarse_map.shape[2]
    small = [
        pltpu.make_async_copy(source, target, sems.at[i])
        for i, (source, target) in enumerate(((neighbours, codes), (coarse_map, groups)))
    ]
    large = [
        pltpu.make_async_copy(tentative, base.at[pl.ds(0, slots)], sems.at[2]),
        pltpu.make_async_copy(inv_diag, scale, sems.at[3]),
    ] + [pltpu.make_async_copy(blocks.at[row], held.at[row], sems.at[4 + row]) for row in range(slots)]
    for copy in small + large:
        copy.start()
    base[slots] = jnp.zeros_like(base[slots])

    here = lax.axis_index("blk")
    odd = lax.rem(here, 2)
    beside = 3 - 2 * odd
    for copy in small:
        copy.wait()
    live = counts[0]
    mine = [groups[0, row, here] for row in range(slots)]
    for offset in range(OFFSETS):
        there = here + (offset - 2)
        there = jnp.where(there < 0, there + cycle, jnp.where(there >= cycle, there - cycle, there))
        if offset in (1, 3):
            first = beside == offset
            panel = jnp.where(first, 1, 2)
            stride = jnp.where(first, NEAR * NCG, FAR * NCG)
        else:
            first = jnp.bool_(offset == 2)
            panel = {2: 0, 0: 0, 4: 1}[offset]
            stride = (NEAR if offset == 2 else FAR) * NCG
        for slot in range(slots):
            other = groups[0, slot, there]
            for row in range(slots):
                at = row * OFFSETS * slots + offset * slots + slot
                word = 256 * (panel * slots + slot) + 65536 * (mine[row] * stride + panel * NCG + other)
                table[at] = word + jnp.where(first, 1 << 30, 0)
    keep = [[jnp.where((mine[slot] == mine[row]) & (slot < live), slot, slots) for slot in range(slots)]
            for row in range(slots)]
    near = jnp.int32(0)
    kept = []
    for row in range(slots):
        for n in range(nnz):
            entry = row * nnz + n
            code = codes[row, n]
            chosen = jnp.int32(slots)
            for slot in range(slots):
                chosen = jnp.where(code == 2 * slots + slot, keep[row][slot], chosen)
            kept.append(chosen)
            word = table[row * OFFSETS * slots + code]
            first = lax.shift_right_logical(word, 30)
            at = jnp.where(first == 1, near, slots * nnz - 1 - entry + near)
            todo[at] = (word & ((1 << 30) - 1)) + entry
            near = near + first
    todo[slots * nnz] = near
    todo[slots * nnz + 1] = odd
    todo[slots * nnz + 2] = lax.axis_index("grp")

    for copy in large[:2]:
        copy.wait()
    width = out.shape[2]
    for row in range(slots):
        large[2 + row].wait()
        total = None
        for n in range(nnz):
            term = jnp.dot(held[row, n], base[kept[row * nnz + n]], preferred_element_type=jnp.float32)
            total = term if total is None else total + term
        factor = jnp.broadcast_to(omega * scale[row : row + 1, :], (width, scale.shape[1])).T
        value = base[row].astype(jnp.float32) - factor * total
        value = jnp.where(row < live, value, 0.0).astype(out.dtype)
        out[row] = value
        flipped[row] = value.T


def prolong_call(counts, *arrays):
    neighbours, coarse_map, blocks, tentative, inv_diag = arrays
    slots, pores, width = tentative.shape
    nnz = neighbours.shape[1]
    arrays = [pltpu.with_memory_space_constraint(x, pltpu.HBM) for x in arrays]
    return pl.pallas_call(
        prolong_kernel,
        out_shape=(
            jax.ShapeDtypeStruct(tentative.shape, tentative.dtype),
            jax.ShapeDtypeStruct((slots, width, pores), tentative.dtype),
            jax.ShapeDtypeStruct((slots * nnz + 8,), jnp.int32),
        ),
        in_specs=[SMEM] + [ANY] * len(arrays),
        out_specs=(VMEM, VMEM, SMEM),
        scratch_shapes=[
            pltpu.VMEM(blocks.shape, blocks.dtype),
            pltpu.VMEM((slots + 1, pores, width), tentative.dtype),
            pltpu.VMEM(inv_diag.shape, inv_diag.dtype),
            pltpu.SMEM(neighbours.shape, jnp.int32),
            pltpu.SMEM(coarse_map.shape, jnp.int32),
            pltpu.SMEM((slots * OFFSETS * slots,), jnp.int32),
            pltpu.SemaphoreType.DMA((4 + slots,)),
        ],
        compiler_params=pltpu.CompilerParams(vmem_limit_bytes=16 << 20),
        cost_estimate=pl.CostEstimate(flops=100_000_000, bytes_accessed=1_000_000, transcendentals=0),
        name="prolong",
    )(counts, *arrays)


def galerkin_kernel(far, layout, parts, nnz, todo, blocks, flipped, *refs):
    slots = flipped.shape[0]
    panels = FAR if far else NEAR
    dests = NCG * panels * NCG
    halo, refs = refs[:panels], refs[panels:]
    carried, refs = refs[: sum(carry for _, carry in layout)], refs[sum(carry for _, carry in layout) :]
    outs, (pool, acc) = refs[: len(layout)], refs[len(layout) :]
    for panel in range(panels):
        for slot in range(slots):
            pool[panel * slots + slot] = halo[panel][slot]
    acc[...] = jnp.zeros_like(acc)
    entries = slots * nnz
    near = todo[entries]
    count = entries - near if far else near

    def some(step, carry):
        grams, places = [], []
        for j in range(nnz):
            at = step * nnz + j
            word = todo[entries - 1 - at if far else at]
            dest = lax.shift_right_logical(word, 16)
            panel = lax.shift_right_logical(word, 8) & 255
            entry = word & 255
            inside = at < count
            places.append(jnp.where(inside, dest, dests))
            panel = jnp.where(inside, panel, 0)
            row = lax.div(entry, nnz)
            pair = jnp.dot(blocks[entry], pool[panel], preferred_element_type=jnp.float32).astype(pool.dtype)
            grams.append(jnp.dot(flipped[row], pair, preferred_element_type=jnp.float32))
        for place, gram in zip(places, grams):
            acc[place] = acc[place] + gram
        return carry

    lax.fori_loop(0, lax.div(count + nnz - 1, nnz), some, 0)

    for (distance, carry), out in zip(layout, outs):
        rows = out.shape[1]
        start = 0
        if parts > 1:
            target = lax.rem(todo[entries + 2] + distance, parts)
            start = pl.multiple_of(target * rows, rows)
        skip = out.shape[0] - dests
        if carry:
            source, carried = carried[0], carried[1:]
            out[pl.ds(0, skip)] = source[...]
        for dest in range(dests):
            out[skip + dest] = acc[dest, pl.ds(start, rows), :].astype(out.dtype)


def galerkin_call(far, layout, parts, todo, blocks, flipped, halo, carried):
    slots, width, pores = flipped.shape
    nnz = blocks.shape[1]
    panels = FAR if far else NEAR
    dests = NCG * panels * NCG
    rows = width // parts
    before = [carried[0].shape[0] if carry else 0 for _, carry in layout]
    return pl.pallas_call(
        functools.partial(galerkin_kernel, far, layout, parts, nnz),
        out_shape=[
            jax.ShapeDtypeStruct((skip + dests, rows, width), flipped.dtype if distance else jnp.float32)
            for (distance, _), skip in zip(layout, before)
        ],
        in_specs=[SMEM, VMEM, VMEM] + [VMEM] * (len(halo) + len(carried)),
        out_specs=[VMEM] * len(layout),
        scratch_shapes=[
            pltpu.VMEM((panels * slots, pores, width), flipped.dtype),
            pltpu.VMEM((dests + 1, width, width), jnp.float32),
        ],
        compiler_params=pltpu.CompilerParams(vmem_limit_bytes=24 << 20),
        cost_estimate=pl.CostEstimate(flops=200_000_000, bytes_accessed=2_000_000, transcendentals=0),
        name="far" if far else "near",
    )(todo, blocks.reshape(slots * nnz, pores, pores), flipped, *halo, *carried)


def finish_kernel(at_odd, nears, fars, boths, todo, *refs):
    near, refs = refs[:nears], refs[nears:]
    far, refs = refs[:fars], refs[fars:]
    both, out = refs[:boths], refs[boths]
    odd = todo[at_odd] == 1
    skip = NCG * NEAR * NCG
    for pieces, panels, first in ((near, NEAR, 0), (far, FAR, skip)):
        for c in range(NCG):
            for panel in range(panels):
                if panels == NEAR:
                    offset = jnp.where(odd, 1, 3) if panel else 2
                else:
                    offset = (0, 4, jnp.where(odd, 3, 1))[panel]
                for c2 in range(NCG):
                    dest = (c * panels + panel) * NCG + c2
                    total = pieces[0][dest].astype(jnp.float32)
                    for piece in pieces[1:]:
                        total = total + piece[dest].astype(jnp.float32)
                    for piece in both:
                        total = total + piece[first + dest].astype(jnp.float32)
                    out[c, offset, c2] = total


def finish_call(at_odd, todo, near, far, both, rows, width):
    return pl.pallas_call(
        functools.partial(finish_kernel, at_odd, len(near), len(far), len(both)),
        out_shape=jax.ShapeDtypeStruct((NCG, OFFSETS, NCG, rows, width), jnp.float32),
        in_specs=[SMEM] + [VMEM] * (len(near) + len(far) + len(both)),
        out_specs=VMEM,
        compiler_params=pltpu.CompilerParams(vmem_limit_bytes=16 << 20),
        cost_estimate=pl.CostEstimate(flops=1_000_000, bytes_accessed=1_500_000, transcendentals=0),
        name="finish",
    )(todo, *near, *far, *both)


def local(blocks, neighbours, tentative, inv_diag, coarse_map, counts):
    parts = lax.axis_size("grp")
    slots, pores, width = tentative.shape
    nnz = neighbours.shape[1]
    own, flipped, todo = prolong_call(
        counts, neighbours, jnp.transpose(coarse_map, (1, 2, 0)), blocks, tentative, inv_diag
    )
    sibling = from_sibling(own)
    behind = from_behind(own, "blk", 2)
    ahead = from_behind(own, "blk", -2)
    across = from_across(own)

    split = parts <= 4
    share = parts if split else 1
    early = EARLY[parts] if split else []
    late = LATE[parts] if split else []
    layout = [(0, False)] + [(d, False) for d in early + late]
    near = galerkin_call(False, layout, share, todo, blocks, flipped, [own, sibling], [])
    near_own, near_early, near_late = near[0], near[1 : 1 + len(early)], near[1 + len(early) :]
    near_early = [from_behind(piece, "grp", d) for piece, d in zip(near_early, early)]
    layout = [(0, False)] + [(d, False) for d in early] + [(d, True) for d in late]
    far = galerkin_call(True, layout, share, todo, blocks, flipped, [behind, ahead, across], near_late)
    if GATE:
        near_early, far = lax.optimization_barrier((near_early, far))
    far_own, far_early, both = far[0], far[1 : 1 + len(early)], far[1 + len(early) :]
    order = [d for d in ORDER[parts]] if split else []
    moved = {d: from_behind(piece, "grp", d) for d, piece in sorted(
        zip(early + late, far_early + both), key=lambda item: order.index(item[0]))}
    far_early = [moved[d] for d in early]
    both = [moved[d] for d in late]
    if not split:
        near_own, far_own = gathered(near_own, parts), gathered(far_own, parts)
    return finish_call(
        slots * nnz + 1, todo, [near_own] + near_early, [far_own] + far_early, both, width // parts, width
    )


GATE = True
EARLY = {1: [], 2: [1], 3: [1], 4: [1, 3]}
LATE = {1: [], 2: [], 3: [2], 4: [2]}
ORDER = {1: [], 2: [1], 3: [1, 2], 4: [2, 1, 3]}


def gathered(whole, parts):
    dests, width, _ = whole.shape
    pieces = whole.astype(jnp.bfloat16).reshape(dests, parts, width // parts, width)
    arrived = lax.all_to_all(pieces, "grp", 1, 1, tiled=True)
    return jnp.sum(arrived.astype(jnp.float32), axis=1)


def solution(mesh):
    return jax.shard_map(
        local,
        mesh=mesh,
        in_specs=(
            P(("blk", "grp"), None, None, None),
            P(("blk", "grp"), None),
            P(("blk", "grp"), None, None),
            P(("blk", "grp"), None),
            P(None, "grp", None),
            P(("blk", "grp")),
        ),
        out_specs=P("blk", None, None, "grp", None),
        check_vma=False,
    )
```

```python
import functools

import jax
import jax.numpy as jnp
from jax import lax
from jax.experimental import pallas as pl
from jax.experimental.pallas import tpu as pltpu
from jax.sharding import PartitionSpec as P

NCG = 2
OFFSETS = 5
NEAR = 2
FAR = 3
omega = 0.6

SMEM = pl.BlockSpec(memory_space=pltpu.SMEM)
VMEM = pl.BlockSpec(memory_space=pltpu.VMEM)
ANY = pl.BlockSpec(memory_space=pltpu.HBM)


def from_behind(block, axis, distance):
    size = lax.axis_size(axis)
    return lax.ppermute(block, axis, [((i - distance) % size, i) for i in range(size)])


def from_sibling(block):
    size = lax.axis_size("blk")
    return lax.ppermute(block, "blk", [(i ^ 1, i) for i in range(size)])


def from_across(block):
    size = lax.axis_size("blk")
    return lax.ppermute(block, "blk", [((i + (1 if i % 2 else -1)) % size, i) for i in range(size)])


def prolong_kernel(counts, neighbours, coarse_map, blocks, tentative, inv_diag, out, flipped, todo,
                   held, base, scale, codes, groups, table, sems):
    slots, nnz = neighbours.shape
    cycle = coarse_map.shape[2]
    small = [
        pltpu.make_async_copy(source, target, sems.at[i])
        for i, (source, target) in enumerate(((neighbours, codes), (coarse_map, groups)))
    ]
    large = [
        pltpu.make_async_copy(tentative, base.at[pl.ds(0, slots)], sems.at[2]),
        pltpu.make_async_copy(inv_diag, scale, sems.at[3]),
    ] + [pltpu.make_async_copy(blocks.at[row], held.at[row], sems.at[4 + row]) for row in range(slots)]
    for copy in small + large:
        copy.start()
    base[slots] = jnp.zeros_like(base[slots])

    here = lax.axis_index("blk")
    odd = lax.rem(here, 2)
    beside = 3 - 2 * odd
    for copy in small:
        copy.wait()
    live = counts[0]
    mine = [groups[0, row, here] for row in range(slots)]
    for offset in range(OFFSETS):
        there = here + (offset - 2)
        there = jnp.where(there < 0, there + cycle, jnp.where(there >= cycle, there - cycle, there))
        if offset in (1, 3):
            first = beside == offset
            panel = jnp.where(first, 1, 2)
            stride = jnp.where(first, NEAR * NCG, FAR * NCG)
        else:
            first = jnp.bool_(offset == 2)
            panel = {2: 0, 0: 0, 4: 1}[offset]
            stride = (NEAR if offset == 2 else FAR) * NCG
        for slot in range(slots):
            other = groups[0, slot, there]
            for row in range(slots):
                at = row * OFFSETS * slots + offset * slots + slot
                word = 256 * (panel * slots + slot) + 65536 * (mine[row] * stride + panel * NCG + other)
                table[at] = word + jnp.where(first, 1 << 30, 0)
    keep = [[jnp.where((mine[slot] == mine[row]) & (slot < live), slot, slots) for slot in range(slots)]
            for row in range(slots)]
    near = jnp.int32(0)
    kept = []
    for row in range(slots):
        for n in range(nnz):
            entry = row * nnz + n
            code = codes[row, n]
            chosen = jnp.int32(slots)
            for slot in range(slots):
                chosen = jnp.where(code == 2 * slots + slot, keep[row][slot], chosen)
            kept.append(chosen)
            word = table[row * OFFSETS * slots + code]
            first = lax.shift_right_logical(word, 30)
            at = jnp.where(first == 1, near, slots * nnz - 1 - entry + near)
            todo[at] = (word & ((1 << 30) - 1)) + entry
            near = near + first
    todo[slots * nnz] = near
    todo[slots * nnz + 1] = odd
    todo[slots * nnz + 2] = lax.axis_index("grp")

    for copy in large[:2]:
        copy.wait()
    width = out.shape[2]
    for row in range(slots):
        large[2 + row].wait()
        total = None
        for n in range(nnz):
            term = jnp.dot(held[row, n], base[kept[row * nnz + n]], preferred_element_type=jnp.float32)
            total = term if total is None else total + term
        factor = jnp.broadcast_to(omega * scale[row : row + 1, :], (width, scale.shape[1])).T
        value = base[row].astype(jnp.float32) - factor * total
        value = jnp.where(row < live, value, 0.0).astype(out.dtype)
        out[row] = value
        flipped[row] = value.T


def prolong_call(counts, *arrays):
    neighbours, coarse_map, blocks, tentative, inv_diag = arrays
    slots, pores, width = tentative.shape
    nnz = neighbours.shape[1]
    arrays = [pltpu.with_memory_space_constraint(x, pltpu.HBM) for x in arrays]
    return pl.pallas_call(
        prolong_kernel,
        out_shape=(
            jax.ShapeDtypeStruct(tentative.shape, tentative.dtype),
            jax.ShapeDtypeStruct((slots, width, pores), tentative.dtype),
            jax.ShapeDtypeStruct((slots * nnz + 8,), jnp.int32),
        ),
        in_specs=[SMEM] + [ANY] * len(arrays),
        out_specs=(VMEM, VMEM, SMEM),
        scratch_shapes=[
            pltpu.VMEM(blocks.shape, blocks.dtype),
            pltpu.VMEM((slots + 1, pores, width), tentative.dtype),
            pltpu.VMEM(inv_diag.shape, inv_diag.dtype),
            pltpu.SMEM(neighbours.shape, jnp.int32),
            pltpu.SMEM(coarse_map.shape, jnp.int32),
            pltpu.SMEM((slots * OFFSETS * slots,), jnp.int32),
            pltpu.SemaphoreType.DMA((4 + slots,)),
        ],
        compiler_params=pltpu.CompilerParams(vmem_limit_bytes=16 << 20),
        cost_estimate=pl.CostEstimate(flops=100_000_000, bytes_accessed=1_000_000, transcendentals=0),
        name="prolong",
    )(counts, *arrays)


def galerkin_kernel(far, layout, parts, nnz, todo, blocks, flipped, *refs):
    slots = flipped.shape[0]
    panels = FAR if far else NEAR
    dests = NCG * panels * NCG
    halo, refs = refs[:panels], refs[panels:]
    carried, refs = refs[: sum(carry for _, carry in layout)], refs[sum(carry for _, carry in layout) :]
    outs, (pool, acc) = refs[: len(layout)], refs[len(layout) :]
    for panel in range(panels):
        for slot in range(slots):
            pool[panel * slots + slot] = halo[panel][slot]
    acc[...] = jnp.zeros_like(acc)
    entries = slots * nnz
    near = todo[entries]
    count = entries - near if far else near

    def some(step, carry):
        grams, places = [], []
        for j in range(nnz):
            at = step * nnz + j
            word = todo[entries - 1 - at if far else at]
            dest = lax.shift_right_logical(word, 16)
            panel = lax.shift_right_logical(word, 8) & 255
            entry = word & 255
            inside = at < count
            places.append(jnp.where(inside, dest, dests))
            panel = jnp.where(inside, panel, 0)
            row = lax.div(entry, nnz)
            pair = jnp.dot(blocks[entry], pool[panel], preferred_element_type=jnp.float32).astype(pool.dtype)
            grams.append(jnp.dot(flipped[row], pair, preferred_element_type=jnp.float32))
        for place, gram in zip(places, grams):
            acc[place] = acc[place] + gram
        return carry

    lax.fori_loop(0, lax.div(count + nnz - 1, nnz), some, 0)

    for (distance, carry), out in zip(layout, outs):
        rows = out.shape[1]
        start = 0
        if parts > 1:
            target = lax.rem(todo[entries + 2] + distance, parts)
            start = pl.multiple_of(target * rows, rows)
        skip = out.shape[0] - dests
        if carry:
            source, carried = carried[0], carried[1:]
            out[pl.ds(0, skip)] = source[...]
        for dest in range(dests):
            out[skip + dest] = acc[dest, pl.ds(start, rows), :].astype(out.dtype)


def galerkin_call(far, layout, parts, todo, blocks, flipped, halo, carried):
    slots, width, pores = flipped.shape
    nnz = blocks.shape[1]
    panels = FAR if far else NEAR
    dests = NCG * panels * NCG
    rows = width // parts
    before = [carried[0].shape[0] if carry else 0 for _, carry in layout]
    return pl.pallas_call(
        functools.partial(galerkin_kernel, far, layout, parts, nnz),
        out_shape=[
            jax.ShapeDtypeStruct((skip + dests, rows, width), flipped.dtype if distance else jnp.float32)
            for (distance, _), skip in zip(layout, before)
        ],
        in_specs=[SMEM, VMEM, VMEM] + [VMEM] * (len(halo) + len(carried)),
        out_specs=[VMEM] * len(layout),
        scratch_shapes=[
            pltpu.VMEM((panels * slots, pores, width), flipped.dtype),
            pltpu.VMEM((dests + 1, width, width), jnp.float32),
        ],
        compiler_params=pltpu.CompilerParams(vmem_limit_bytes=24 << 20),
        cost_estimate=pl.CostEstimate(flops=200_000_000, bytes_accessed=2_000_000, transcendentals=0),
        name="far" if far else "near",
    )(todo, blocks.reshape(slots * nnz, pores, pores), flipped, *halo, *carried)


def finish_kernel(at_odd, nears, fars, boths, todo, *refs):
    near, refs = refs[:nears], refs[nears:]
    far, refs = refs[:fars], refs[fars:]
    both, out = refs[:boths], refs[boths]
    odd = todo[at_odd] == 1
    skip = NCG * NEAR * NCG
    for pieces, panels, first in ((near, NEAR, 0), (far, FAR, skip)):
        for c in range(NCG):
            for panel in range(panels):
                if panels == NEAR:
                    offset = jnp.where(odd, 1, 3) if panel else 2
                else:
                    offset = (0, 4, jnp.where(odd, 3, 1))[panel]
                for c2 in range(NCG):
                    dest = (c * panels + panel) * NCG + c2
                    total = pieces[0][dest].astype(jnp.float32)
                    for piece in pieces[1:]:
                        total = total + piece[dest].astype(jnp.float32)
                    for piece in both:
                        total = total + piece[first + dest].astype(jnp.float32)
                    out[c, offset, c2] = total


def finish_call(at_odd, todo, near, far, both, rows, width):
    return pl.pallas_call(
        functools.partial(finish_kernel, at_odd, len(near), len(far), len(both)),
        out_shape=jax.ShapeDtypeStruct((NCG, OFFSETS, NCG, rows, width), jnp.float32),
        in_specs=[SMEM] + [VMEM] * (len(near) + len(far) + len(both)),
        out_specs=VMEM,
        compiler_params=pltpu.CompilerParams(vmem_limit_bytes=16 << 20),
        cost_estimate=pl.CostEstimate(flops=1_000_000, bytes_accessed=1_500_000, transcendentals=0),
        name="finish",
    )(todo, *near, *far, *both)


def local(blocks, neighbours, tentative, inv_diag, coarse_map, counts):
    parts = lax.axis_size("grp")
    slots, pores, width = tentative.shape
    nnz = neighbours.shape[1]
    own, flipped, todo = prolong_call(
        counts, neighbours, jnp.transpose(coarse_map, (1, 2, 0)), blocks, tentative, inv_diag
    )
    sibling = from_sibling(own)
    behind = from_behind(own, "blk", 2)
    ahead = from_behind(own, "blk", -2)
    across = from_across(own)

    split = parts <= 4
    share = parts if split else 1
    early = EARLY[parts] if split else []
    late = LATE[parts] if split else []
    layout = [(0, False)] + [(d, False) for d in early + late]
    near = galerkin_call(False, layout, share, todo, blocks, flipped, [own, sibling], [])
    near_own, near_early, near_late = near[0], near[1 : 1 + len(early)], near[1 + len(early) :]
    near_early = [from_behind(piece, "grp", d) for piece, d in zip(near_early, early)]
    layout = [(0, False)] + [(d, False) for d in early] + [(d, True) for d in late]
    far = galerkin_call(True, layout, share, todo, blocks, flipped, [behind, ahead, across], near_late)
    if near_early:
        *far, last = far
        near_early, last = lax.optimization_barrier((near_early, last))
        far = [*far, last]
    far_own, far_early, both = far[0], far[1 : 1 + len(early)], far[1 + len(early) :]
    order = [d for d in ORDER[parts]] if split else []
    moved = {d: from_behind(piece, "grp", d) for d, piece in sorted(
        zip(early + late, far_early + both), key=lambda item: order.index(item[0]))}
    far_early = [moved[d] for d in early]
    both = [moved[d] for d in late]
    if not split:
        near_own, far_own = gathered(near_own, parts), gathered(far_own, parts)
    return finish_call(
        slots * nnz + 1, todo, [near_own] + near_early, [far_own] + far_early, both, width // parts, width
    )


EARLY = {1: [], 2: [1], 3: [1], 4: [2, 1, 3]}
LATE = {1: [], 2: [], 3: [2], 4: []}
ORDER = {1: [], 2: [1], 3: [1, 2], 4: [2, 1, 3]}


def gathered(whole, parts):
    dests, width, _ = whole.shape
    pieces = whole.astype(jnp.bfloat16).reshape(dests, parts, width // parts, width)
    arrived = lax.all_to_all(pieces, "grp", 1, 1, tiled=True)
    return jnp.sum(arrived.astype(jnp.float32), axis=1)


def solution(mesh):
    return jax.shard_map(
        local,
        mesh=mesh,
        in_specs=(
            P(("blk", "grp"), None, None, None),
            P(("blk", "grp"), None),
            P(("blk", "grp"), None, None),
            P(("blk", "grp"), None),
            P(None, "grp", None),
            P(("blk", "grp")),
        ),
        out_specs=P("blk", None, None, "grp", None),
        check_vma=False,
    )
```

```python
import functools

import jax
import jax.numpy as jnp
from jax import lax
from jax.experimental import pallas as pl
from jax.experimental.pallas import tpu as pltpu
from jax.sharding import PartitionSpec as P

NCG = 2
OFFSETS = 5
NEAR = 2
FAR = 3
omega = 0.6

SMEM = pl.BlockSpec(memory_space=pltpu.SMEM)
VMEM = pl.BlockSpec(memory_space=pltpu.VMEM)
ANY = pl.BlockSpec(memory_space=pltpu.HBM)


def from_behind(block, axis, distance):
    size = lax.axis_size(axis)
    return lax.ppermute(block, axis, [((i - distance) % size, i) for i in range(size)])


def from_sibling(block):
    size = lax.axis_size("blk")
    return lax.ppermute(block, "blk", [(i ^ 1, i) for i in range(size)])


def from_across(block):
    size = lax.axis_size("blk")
    return lax.ppermute(block, "blk", [((i + (1 if i % 2 else -1)) % size, i) for i in range(size)])


def prolong_kernel(counts, neighbours, coarse_map, blocks, tentative, inv_diag, out, flipped, todo,
                   held, base, scale, codes, groups, table, sems):
    slots, nnz = neighbours.shape
    cycle = coarse_map.shape[2]
    small = [
        pltpu.make_async_copy(source, target, sems.at[i])
        for i, (source, target) in enumerate(((neighbours, codes), (coarse_map, groups)))
    ]
    large = [
        pltpu.make_async_copy(tentative, base.at[pl.ds(0, slots)], sems.at[2]),
        pltpu.make_async_copy(inv_diag, scale, sems.at[3]),
    ] + [pltpu.make_async_copy(blocks.at[row], held.at[row], sems.at[4 + row]) for row in range(slots)]
    for copy in small + large:
        copy.start()
    base[slots] = jnp.zeros_like(base[slots])

    here = lax.axis_index("blk")
    odd = lax.rem(here, 2)
    beside = 3 - 2 * odd
    for copy in small:
        copy.wait()
    live = counts[0]
    mine = [groups[0, row, here] for row in range(slots)]
    for offset in range(OFFSETS):
        there = here + (offset - 2)
        there = jnp.where(there < 0, there + cycle, jnp.where(there >= cycle, there - cycle, there))
        if offset in (1, 3):
            first = beside == offset
            panel = jnp.where(first, 1, 2)
            stride = jnp.where(first, NEAR * NCG, FAR * NCG)
        else:
            first = jnp.bool_(offset == 2)
            panel = {2: 0, 0: 0, 4: 1}[offset]
            stride = (NEAR if offset == 2 else FAR) * NCG
        for slot in range(slots):
            other = groups[0, slot, there]
            for row in range(slots):
                at = row * OFFSETS * slots + offset * slots + slot
                word = 256 * (panel * slots + slot) + 65536 * (mine[row] * stride + panel * NCG + other)
                table[at] = word + jnp.where(first, 1 << 30, 0)
    keep = [[jnp.where((mine[slot] == mine[row]) & (slot < live), slot, slots) for slot in range(slots)]
            for row in range(slots)]
    near = jnp.int32(0)
    kept = []
    for row in range(slots):
        for n in range(nnz):
            entry = row * nnz + n
            code = codes[row, n]
            chosen = jnp.int32(slots)
            for slot in range(slots):
                chosen = jnp.where(code == 2 * slots + slot, keep[row][slot], chosen)
            kept.append(chosen)
            word = table[row * OFFSETS * slots + code]
            first = lax.shift_right_logical(word, 30)
            at = jnp.where(first == 1, near, slots * nnz - 1 - entry + near)
            todo[at] = (word & ((1 << 30) - 1)) + entry
            near = near + first
    todo[slots * nnz] = near

    for copy in large[:2]:
        copy.wait()
    width = out.shape[2]
    for row in range(slots):
        large[2 + row].wait()
        total = None
        for n in range(nnz):
            term = jnp.dot(held[row, n], base[kept[row * nnz + n]], preferred_element_type=jnp.float32)
            total = term if total is None else total + term
        factor = jnp.broadcast_to(omega * scale[row : row + 1, :], (width, scale.shape[1])).T
        value = base[row].astype(jnp.float32) - factor * total
        value = jnp.where(row < live, value, 0.0).astype(out.dtype)
        out[row] = value
        flipped[row] = value.T


def prolong_call(counts, *arrays):
    neighbours, coarse_map, blocks, tentative, inv_diag = arrays
    slots, pores, width = tentative.shape
    nnz = neighbours.shape[1]
    arrays = [pltpu.with_memory_space_constraint(x, pltpu.HBM) for x in arrays]
    return pl.pallas_call(
        prolong_kernel,
        out_shape=(
            jax.ShapeDtypeStruct(tentative.shape, tentative.dtype),
            jax.ShapeDtypeStruct((slots, width, pores), tentative.dtype),
            jax.ShapeDtypeStruct((slots * nnz + 8,), jnp.int32),
        ),
        in_specs=[SMEM] + [ANY] * len(arrays),
        out_specs=(VMEM, VMEM, SMEM),
        scratch_shapes=[
            pltpu.VMEM(blocks.shape, blocks.dtype),
            pltpu.VMEM((slots + 1, pores, width), tentative.dtype),
            pltpu.VMEM(inv_diag.shape, inv_diag.dtype),
            pltpu.SMEM(neighbours.shape, jnp.int32),
            pltpu.SMEM(coarse_map.shape, jnp.int32),
            pltpu.SMEM((slots * OFFSETS * slots,), jnp.int32),
            pltpu.SemaphoreType.DMA((4 + slots,)),
        ],
        compiler_params=pltpu.CompilerParams(vmem_limit_bytes=16 << 20),
        cost_estimate=pl.CostEstimate(flops=100_000_000, bytes_accessed=1_000_000, transcendentals=0),
        name="prolong",
    )(counts, *arrays)


def galerkin_kernel(far, layout, parts, nnz, todo, blocks, flipped, *refs):
    slots = flipped.shape[0]
    panels = FAR if far else NEAR
    dests = NCG * panels * NCG
    halo, refs = refs[:panels], refs[panels:]
    carried, refs = refs[: sum(carry for _, carry in layout)], refs[sum(carry for _, carry in layout) :]
    outs, (pool, acc) = refs[: len(layout)], refs[len(layout) :]
    for panel in range(panels):
        for slot in range(slots):
            pool[panel * slots + slot] = halo[panel][slot]
    acc[...] = jnp.zeros_like(acc)
    entries = slots * nnz
    near = todo[entries]
    count = entries - near if far else near

    def some(step, carry):
        grams, places = [], []
        for j in range(nnz):
            at = step * nnz + j
            word = todo[entries - 1 - at if far else at]
            dest = lax.shift_right_logical(word, 16)
            panel = lax.shift_right_logical(word, 8) & 255
            entry = word & 255
            inside = at < count
            places.append(jnp.where(inside, dest, dests))
            panel = jnp.where(inside, panel, 0)
            row = lax.div(entry, nnz)
            pair = jnp.dot(blocks[entry], pool[panel], preferred_element_type=jnp.float32).astype(pool.dtype)
            grams.append(jnp.dot(flipped[row], pair, preferred_element_type=jnp.float32))
        for place, gram in zip(places, grams):
            acc[place] = acc[place] + gram
        return carry

    lax.fori_loop(0, lax.div(count + nnz - 1, nnz), some, 0)

    for (distance, carry), out in zip(layout, outs):
        rows = out.shape[1]
        start = 0
        if parts > 1:
            target = lax.rem(lax.axis_index("grp") + distance, parts)
            start = pl.multiple_of(target * rows, rows)
        skip = out.shape[0] - dests
        if carry:
            source, carried = carried[0], carried[1:]
            out[pl.ds(0, skip)] = source[...]
        for dest in range(dests):
            out[skip + dest] = acc[dest, pl.ds(start, rows), :].astype(out.dtype)


def galerkin_call(far, layout, parts, todo, blocks, flipped, halo, carried):
    slots, width, pores = flipped.shape
    nnz = blocks.shape[1]
    panels = FAR if far else NEAR
    dests = NCG * panels * NCG
    rows = width // parts
    before = [carried[0].shape[0] if carry else 0 for _, carry in layout]
    return pl.pallas_call(
        functools.partial(galerkin_kernel, far, layout, parts, nnz),
        out_shape=[
            jax.ShapeDtypeStruct((skip + dests, rows, width), flipped.dtype if distance else jnp.float32)
            for (distance, _), skip in zip(layout, before)
        ],
        in_specs=[SMEM, VMEM, VMEM] + [VMEM] * (len(halo) + len(carried)),
        out_specs=[VMEM] * len(layout),
        scratch_shapes=[
            pltpu.VMEM((panels * slots, pores, width), flipped.dtype),
            pltpu.VMEM((dests + 1, width, width), jnp.float32),
        ],
        compiler_params=pltpu.CompilerParams(vmem_limit_bytes=24 << 20),
        cost_estimate=pl.CostEstimate(flops=200_000_000, bytes_accessed=2_000_000, transcendentals=0),
        name="far" if far else "near",
    )(todo, blocks.reshape(slots * nnz, pores, pores), flipped, *halo, *carried)


def finish_kernel(nears, fars, boths, *refs):
    near, refs = refs[:nears], refs[nears:]
    far, refs = refs[:fars], refs[fars:]
    both, (out, held, sem) = refs[:boths], refs[boths:]
    odd = lax.rem(lax.axis_index("blk"), 2) == 1
    skip = NCG * NEAR * NCG
    for pieces, panels, first in ((near, NEAR, 0), (far, FAR, skip)):
        for c in range(NCG):
            for panel in range(panels):
                if panels == NEAR:
                    offset = jnp.where(odd, 1, 3) if panel else 2
                else:
                    offset = (0, 4, jnp.where(odd, 3, 1))[panel]
                base = (c * panels + panel) * NCG
                for c2 in range(NCG):
                    dest = base + c2
                    total = pieces[0][dest].astype(jnp.float32)
                    for piece in pieces[1:]:
                        total = total + piece[dest].astype(jnp.float32)
                    for piece in both:
                        total = total + piece[first + dest].astype(jnp.float32)
                    held[first + dest] = total
                pltpu.make_async_copy(held.at[pl.ds(first + base, NCG)], out.at[c, offset], sem).start()
    pltpu.make_async_copy(held, held, sem).wait()


def finish_call(near, far, both, rows, width):
    return pl.pallas_call(
        functools.partial(finish_kernel, len(near), len(far), len(both)),
        out_shape=jax.ShapeDtypeStruct((NCG, OFFSETS, NCG, rows, width), jnp.float32),
        in_specs=[VMEM] * (len(near) + len(far) + len(both)),
        out_specs=ANY,
        scratch_shapes=[
            pltpu.VMEM((NCG * OFFSETS * NCG, rows, width), jnp.float32),
            pltpu.SemaphoreType.DMA,
        ],
        compiler_params=pltpu.CompilerParams(vmem_limit_bytes=16 << 20),
        cost_estimate=pl.CostEstimate(flops=1_000_000, bytes_accessed=1_500_000, transcendentals=0),
        name="finish",
    )(*near, *far, *both)


def local(blocks, neighbours, tentative, inv_diag, coarse_map, counts):
    parts = lax.axis_size("grp")
    slots, pores, width = tentative.shape
    nnz = neighbours.shape[1]
    own, flipped, todo = prolong_call(
        counts, neighbours, jnp.transpose(coarse_map, (1, 2, 0)), blocks, tentative, inv_diag
    )
    sibling = from_sibling(own)
    behind = from_behind(own, "blk", 2)
    ahead = from_behind(own, "blk", -2)
    across = from_across(own)

    split = parts <= 4
    share = parts if split else 1
    early = EARLY[parts] if split else []
    late = LATE[parts] if split else []
    layout = [(0, False)] + [(d, False) for d in early + late]
    near = galerkin_call(False, layout, share, todo, blocks, flipped, [own, sibling], [])
    near_own, near_early, near_late = near[0], near[1 : 1 + len(early)], near[1 + len(early) :]
    near_early = [from_behind(piece, "grp", d) for piece, d in zip(near_early, early)]
    layout = [(0, False)] + [(d, False) for d in early] + [(d, True) for d in late]
    far = galerkin_call(True, layout, share, todo, blocks, flipped, [behind, ahead, across], near_late)
    if near_early:
        *far, last = far
        near_early, last = lax.optimization_barrier((near_early, last))
        far = [*far, last]
    far_own, far_early, both = far[0], far[1 : 1 + len(early)], far[1 + len(early) :]
    order = [d for d in ORDER[parts]] if split else []
    moved = {d: from_behind(piece, "grp", d) for d, piece in sorted(
        zip(early + late, far_early + both), key=lambda item: order.index(item[0]))}
    far_early = [moved[d] for d in early]
    both = [moved[d] for d in late]
    if not split:
        near_own, far_own = gathered(near_own, parts), gathered(far_own, parts)
    return finish_call(
        [near_own] + near_early, [far_own] + far_early, both, width // parts, width
    )


EARLY = {1: [], 2: [1], 3: [1], 4: [2, 1, 3]}
LATE = {1: [], 2: [], 3: [2], 4: []}
ORDER = {1: [], 2: [1], 3: [1, 2], 4: [2, 1, 3]}


def gathered(whole, parts):
    dests, width, _ = whole.shape
    pieces = whole.astype(jnp.bfloat16).reshape(dests, parts, width // parts, width)
    arrived = lax.all_to_all(pieces, "grp", 1, 1, tiled=True)
    return jnp.sum(arrived.astype(jnp.float32), axis=1)


def solution(mesh):
    return jax.shard_map(
        local,
        mesh=mesh,
        in_specs=(
            P(("blk", "grp"), None, None, None),
            P(("blk", "grp"), None),
            P(("blk", "grp"), None, None),
            P(("blk", "grp"), None),
            P(None, "grp", None),
            P(("blk", "grp")),
        ),
        out_specs=P("blk", None, None, "grp", None),
        check_vma=False,
    )
```

```python
import functools

import jax
import jax.numpy as jnp
from jax import lax
from jax.experimental import pallas as pl
from jax.experimental.pallas import tpu as pltpu
from jax.sharding import PartitionSpec as P

NCG = 2
OFFSETS = 5
NEAR = 2
FAR = 3
omega = 0.6

SMEM = pl.BlockSpec(memory_space=pltpu.SMEM)
VMEM = pl.BlockSpec(memory_space=pltpu.VMEM)
ANY = pl.BlockSpec(memory_space=pltpu.HBM)


def from_behind(block, axis, distance):
    size = lax.axis_size(axis)
    return lax.ppermute(block, axis, [((i - distance) % size, i) for i in range(size)])


def from_sibling(block):
    size = lax.axis_size("blk")
    return lax.ppermute(block, "blk", [(i ^ 1, i) for i in range(size)])


def from_across(block):
    size = lax.axis_size("blk")
    return lax.ppermute(block, "blk", [((i + (1 if i % 2 else -1)) % size, i) for i in range(size)])


def prolong_kernel(counts, neighbours, coarse_map, blocks, tentative, inv_diag, out, flipped, todo,
                   held, base, scale, codes, groups, table, sems):
    slots, nnz = neighbours.shape
    cycle = coarse_map.shape[2]
    small = [
        pltpu.make_async_copy(source, target, sems.at[i])
        for i, (source, target) in enumerate(((neighbours, codes), (coarse_map, groups)))
    ]
    large = [
        pltpu.make_async_copy(tentative, base.at[pl.ds(0, slots)], sems.at[2]),
        pltpu.make_async_copy(inv_diag, scale, sems.at[3]),
    ] + [pltpu.make_async_copy(blocks, held, sems.at[4])]
    for copy in small + large:
        copy.start()
    base[slots] = jnp.zeros_like(base[slots])

    here = lax.axis_index("blk")
    odd = lax.rem(here, 2)
    beside = 3 - 2 * odd
    for copy in small:
        copy.wait()
    live = counts[0]
    mine = [groups[0, row, here] for row in range(slots)]
    for offset in range(OFFSETS):
        there = here + (offset - 2)
        there = jnp.where(there < 0, there + cycle, jnp.where(there >= cycle, there - cycle, there))
        if offset in (1, 3):
            first = beside == offset
            panel = jnp.where(first, 1, 2)
            stride = jnp.where(first, NEAR * NCG, FAR * NCG)
        else:
            first = jnp.bool_(offset == 2)
            panel = {2: 0, 0: 0, 4: 1}[offset]
            stride = (NEAR if offset == 2 else FAR) * NCG
        for slot in range(slots):
            other = groups[0, slot, there]
            for row in range(slots):
                at = row * OFFSETS * slots + offset * slots + slot
                word = 256 * (panel * slots + slot) + 65536 * (mine[row] * stride + panel * NCG + other)
                table[at] = word + jnp.where(first, 1 << 30, 0)
    keep = [[jnp.where((mine[slot] == mine[row]) & (slot < live), slot, slots) for slot in range(slots)]
            for row in range(slots)]
    near = jnp.int32(0)
    kept = []
    for row in range(slots):
        for n in range(nnz):
            entry = row * nnz + n
            code = codes[row, n]
            chosen = jnp.int32(slots)
            for slot in range(slots):
                chosen = jnp.where(code == 2 * slots + slot, keep[row][slot], chosen)
            kept.append(chosen)
            word = table[row * OFFSETS * slots + code]
            first = lax.shift_right_logical(word, 30)
            at = jnp.where(first == 1, near, slots * nnz - 1 - entry + near)
            todo[at] = (word & ((1 << 30) - 1)) + entry
            near = near + first
    todo[slots * nnz] = near

    for copy in large[:2]:
        copy.wait()
    width = out.shape[2]
    for row in range(slots):
        if row == 0:
            large[2].wait()
        total = None
        for n in range(nnz):
            term = jnp.dot(held[row, n], base[kept[row * nnz + n]], preferred_element_type=jnp.float32)
            total = term if total is None else total + term
        factor = jnp.broadcast_to(omega * scale[row : row + 1, :], (width, scale.shape[1])).T
        value = base[row].astype(jnp.float32) - factor * total
        value = jnp.where(row < live, value, 0.0).astype(out.dtype)
        out[row] = value
        flipped[row] = value.T


def prolong_call(counts, *arrays):
    neighbours, coarse_map, blocks, tentative, inv_diag = arrays
    slots, pores, width = tentative.shape
    nnz = neighbours.shape[1]
    arrays = [pltpu.with_memory_space_constraint(x, pltpu.HBM) for x in arrays]
    return pl.pallas_call(
        prolong_kernel,
        out_shape=(
            jax.ShapeDtypeStruct(tentative.shape, tentative.dtype),
            jax.ShapeDtypeStruct((slots, width, pores), tentative.dtype),
            jax.ShapeDtypeStruct((slots * nnz + 8,), jnp.int32),
        ),
        in_specs=[SMEM] + [ANY] * len(arrays),
        out_specs=(VMEM, VMEM, SMEM),
        scratch_shapes=[
            pltpu.VMEM(blocks.shape, blocks.dtype),
            pltpu.VMEM((slots + 1, pores, width), tentative.dtype),
            pltpu.VMEM(inv_diag.shape, inv_diag.dtype),
            pltpu.SMEM(neighbours.shape, jnp.int32),
            pltpu.SMEM(coarse_map.shape, jnp.int32),
            pltpu.SMEM((slots * OFFSETS * slots,), jnp.int32),
            pltpu.SemaphoreType.DMA((5,)),
        ],
        compiler_params=pltpu.CompilerParams(vmem_limit_bytes=16 << 20),
        cost_estimate=pl.CostEstimate(flops=100_000_000, bytes_accessed=1_000_000, transcendentals=0),
        name="prolong",
    )(counts, *arrays)


def galerkin_kernel(far, layout, parts, nnz, words, blocks, flipped, *refs):
    slots = flipped.shape[0]
    panels = FAR if far else NEAR
    dests = NCG * panels * NCG
    halo, refs = refs[:panels], refs[panels:]
    *refs, todo, sem = refs
    list_copy = pltpu.make_async_copy(words, todo, sem)
    list_copy.start()
    carried, refs = refs[: sum(carry for _, carry in layout)], refs[sum(carry for _, carry in layout) :]
    outs, (pool, acc) = refs[: len(layout)], refs[len(layout) :]
    for panel in range(panels):
        for slot in range(slots):
            pool[panel * slots + slot] = halo[panel][slot]
    acc[...] = jnp.zeros_like(acc)
    entries = slots * nnz
    list_copy.wait()
    near = todo[entries]
    count = entries - near if far else near

    batch = nnz

    def some(step, carry):
        grams, places = [], []
        for j in range(batch):
            at = step * batch + j
            word = todo[entries - 1 - at if far else at]
            dest = lax.shift_right_logical(word, 16)
            panel = lax.shift_right_logical(word, 8) & 255
            entry = word & 255
            inside = at < count
            places.append(jnp.where(inside, dest, dests))
            panel = jnp.where(inside, panel, 0)
            row = lax.div(entry, nnz)
            pair = jnp.dot(blocks[entry], pool[panel], preferred_element_type=jnp.float32).astype(pool.dtype)
            grams.append(jnp.dot(flipped[row], pair, preferred_element_type=jnp.float32))
        for place, gram in zip(places, grams):
            acc[place] = acc[place] + gram
        return carry

    if far:
        for step in range(entries // batch):
            some(step, 0)
    else:
        lax.fori_loop(0, lax.div(count + batch - 1, batch), some, 0)

    for (distance, carry), out in zip(layout, outs):
        rows = out.shape[1]
        start = 0
        if parts > 1:
            target = lax.rem(lax.axis_index("grp") + distance, parts)
            start = pl.multiple_of(target * rows, rows)
        skip = out.shape[0] - dests
        if carry:
            source, carried = carried[0], carried[1:]
            out[pl.ds(0, skip)] = source[...]
        for dest in range(dests):
            out[skip + dest] = acc[dest, pl.ds(start, rows), :].astype(out.dtype)


def galerkin_call(far, layout, parts, todo, blocks, flipped, halo, carried):
    slots, width, pores = flipped.shape
    nnz = blocks.shape[1]
    panels = FAR if far else NEAR
    dests = NCG * panels * NCG
    rows = width // parts
    before = [carried[0].shape[0] if carry else 0 for _, carry in layout]
    return pl.pallas_call(
        functools.partial(galerkin_kernel, far, layout, parts, nnz),
        out_shape=[
            jax.ShapeDtypeStruct((skip + dests, rows, width), flipped.dtype if distance else jnp.float32)
            for (distance, _), skip in zip(layout, before)
        ],
        in_specs=[pl.BlockSpec(memory_space=pl.ANY), VMEM, VMEM] + [VMEM] * (len(halo) + len(carried)),
        out_specs=[VMEM] * len(layout),
        scratch_shapes=[
            pltpu.VMEM((panels * slots, pores, width), flipped.dtype),
            pltpu.VMEM((dests + 1, width, width), jnp.float32),
            pltpu.SMEM(todo.shape, jnp.int32),
            pltpu.SemaphoreType.DMA,
        ],
        compiler_params=pltpu.CompilerParams(vmem_limit_bytes=24 << 20),
        cost_estimate=pl.CostEstimate(flops=200_000_000, bytes_accessed=2_000_000, transcendentals=0),
        name="far" if far else "near",
    )(todo, blocks.reshape(slots * nnz, pores, pores), flipped, *halo, *carried)


def finish_kernel(nears, fars, boths, *refs):
    near, refs = refs[:nears], refs[nears:]
    far, refs = refs[:fars], refs[fars:]
    both, (out, held, sem) = refs[:boths], refs[boths:]
    odd = lax.rem(lax.axis_index("blk"), 2) == 1
    skip = NCG * NEAR * NCG
    for pieces, panels, first in ((near, NEAR, 0), (far, FAR, skip)):
        for c in range(NCG):
            for panel in range(panels):
                if panels == NEAR:
                    offset = jnp.where(odd, 1, 3) if panel else 2
                else:
                    offset = (0, 4, jnp.where(odd, 3, 1))[panel]
                base = (c * panels + panel) * NCG
                for c2 in range(NCG):
                    dest = base + c2
                    total = pieces[0][dest].astype(jnp.float32)
                    for piece in pieces[1:]:
                        total = total + piece[dest].astype(jnp.float32)
                    for piece in both:
                        total = total + piece[first + dest].astype(jnp.float32)
                    held[first + dest] = total
                pltpu.make_async_copy(held.at[pl.ds(first + base, NCG)], out.at[c, offset], sem).start()
    pltpu.make_async_copy(held, held, sem).wait()


def finish_call(near, far, both, rows, width):
    return pl.pallas_call(
        functools.partial(finish_kernel, len(near), len(far), len(both)),
        out_shape=jax.ShapeDtypeStruct((NCG, OFFSETS, NCG, rows, width), jnp.float32),
        in_specs=[VMEM] * (len(near) + len(far) + len(both)),
        out_specs=ANY,
        scratch_shapes=[
            pltpu.VMEM((NCG * OFFSETS * NCG, rows, width), jnp.float32),
            pltpu.SemaphoreType.DMA,
        ],
        compiler_params=pltpu.CompilerParams(vmem_limit_bytes=16 << 20),
        cost_estimate=pl.CostEstimate(flops=1_000_000, bytes_accessed=1_500_000, transcendentals=0),
        name="finish",
    )(*near, *far, *both)


def local(blocks, neighbours, tentative, inv_diag, coarse_map, counts):
    parts = lax.axis_size("grp")
    slots, pores, width = tentative.shape
    nnz = neighbours.shape[1]
    own, flipped, todo = prolong_call(
        counts, neighbours, jnp.transpose(coarse_map, (1, 2, 0)), blocks, tentative, inv_diag
    )
    sibling = from_sibling(own)
    behind = from_behind(own, "blk", 2)
    ahead = from_behind(own, "blk", -2)
    across = from_across(own)

    split = parts <= 4
    share = parts if split else 1
    early = EARLY[parts] if split else []
    late = LATE[parts] if split else []
    layout = [(0, False)] + [(d, False) for d in early + late]
    near = galerkin_call(False, layout, share, todo, blocks, flipped, [own, sibling], [])
    near_own, near_early, near_late = near[0], near[1 : 1 + len(early)], near[1 + len(early) :]
    near_early = [from_behind(piece, "grp", d) for piece, d in zip(near_early, early)]
    layout = [(0, False)] + [(d, False) for d in early] + [(d, True) for d in late]
    far = galerkin_call(True, layout, share, todo, blocks, flipped, [behind, ahead, across], near_late)
    if near_early:
        *far, last = far
        near_early, last = lax.optimization_barrier((near_early, last))
        far = [*far, last]
    far_own, far_early, both = far[0], far[1 : 1 + len(early)], far[1 + len(early) :]
    order = [d for d in ORDER[parts]] if split else []
    moved = {d: from_behind(piece, "grp", d) for d, piece in sorted(
        zip(early + late, far_early + both), key=lambda item: order.index(item[0]))}
    far_early = [moved[d] for d in early]
    both = [moved[d] for d in late]
    if not split:
        near_own, far_own = gathered(near_own, parts), gathered(far_own, parts)
    return finish_call(
        [near_own] + near_early, [far_own] + far_early, both, width // parts, width
    )


EARLY = {1: [], 2: [1], 3: [1], 4: [2, 1, 3]}
LATE = {1: [], 2: [], 3: [2], 4: []}
ORDER = {1: [], 2: [1], 3: [1, 2], 4: [2, 1, 3]}


def gathered(whole, parts):
    dests, width, _ = whole.shape
    pieces = whole.astype(jnp.bfloat16).reshape(dests, parts, width // parts, width)
    arrived = lax.all_to_all(pieces, "grp", 1, 1, tiled=True)
    return jnp.sum(arrived.astype(jnp.float32), axis=1)


def solution(mesh):
    return jax.shard_map(
        local,
        mesh=mesh,
        in_specs=(
            P(("blk", "grp"), None, None, None),
            P(("blk", "grp"), None),
            P(("blk", "grp"), None, None),
            P(("blk", "grp"), None),
            P(None, "grp", None),
            P(("blk", "grp")),
        ),
        out_specs=P("blk", None, None, "grp", None),
        check_vma=False,
    )
```

```python
import functools

import jax
import jax.numpy as jnp
from jax import lax
from jax.experimental import pallas as pl
from jax.experimental.pallas import tpu as pltpu
from jax.sharding import PartitionSpec as P

NCG = 2
OFFSETS = 5
NEAR = 2
FAR = 3
omega = 0.6

SMEM = pl.BlockSpec(memory_space=pltpu.SMEM)
VMEM = pl.BlockSpec(memory_space=pltpu.VMEM)
ANY = pl.BlockSpec(memory_space=pltpu.HBM)


def from_behind(block, axis, distance):
    size = lax.axis_size(axis)
    return lax.ppermute(block, axis, [((i - distance) % size, i) for i in range(size)])


def from_partner(block, distance):
    size = lax.axis_size("grp")
    return lax.ppermute(block, "grp", [(i ^ distance, i) for i in range(size)])


def from_sibling(block):
    size = lax.axis_size("blk")
    return lax.ppermute(block, "blk", [(i ^ 1, i) for i in range(size)])


def from_across(block):
    size = lax.axis_size("blk")
    return lax.ppermute(block, "blk", [((i + (1 if i % 2 else -1)) % size, i) for i in range(size)])


def prolong_kernel(counts, neighbours, coarse_map, blocks, tentative, inv_diag, out, flipped, todo,
                   held, base, scale, codes, groups, table, sems):
    slots, nnz = neighbours.shape
    cycle = coarse_map.shape[2]
    small = [
        pltpu.make_async_copy(source, target, sems.at[i])
        for i, (source, target) in enumerate(((neighbours, codes), (coarse_map, groups)))
    ]
    large = [
        pltpu.make_async_copy(tentative, base.at[pl.ds(0, slots)], sems.at[2]),
        pltpu.make_async_copy(inv_diag, scale, sems.at[3]),
    ] + [pltpu.make_async_copy(blocks, held, sems.at[4])]
    for copy in small + large:
        copy.start()
    base[slots] = jnp.zeros_like(base[slots])

    here = lax.axis_index("blk")
    odd = lax.rem(here, 2)
    beside = 3 - 2 * odd
    for copy in small:
        copy.wait()
    live = counts[0]
    mine = [groups[0, row, here] for row in range(slots)]
    for offset in range(OFFSETS):
        there = here + (offset - 2)
        there = jnp.where(there < 0, there + cycle, jnp.where(there >= cycle, there - cycle, there))
        if offset in (1, 3):
            first = beside == offset
            panel = jnp.where(first, 1, 2)
            stride = jnp.where(first, NEAR * NCG, FAR * NCG)
        else:
            first = jnp.bool_(offset == 2)
            panel = {2: 0, 0: 0, 4: 1}[offset]
            stride = (NEAR if offset == 2 else FAR) * NCG
        for slot in range(slots):
            other = groups[0, slot, there]
            for row in range(slots):
                at = row * OFFSETS * slots + offset * slots + slot
                word = 256 * (panel * slots + slot) + 65536 * (mine[row] * stride + panel * NCG + other)
                table[at] = word + jnp.where(first, 1 << 30, 0)
    keep = [[jnp.where((mine[slot] == mine[row]) & (slot < live), slot, slots) for slot in range(slots)]
            for row in range(slots)]
    near = jnp.int32(0)
    kept = []
    for row in range(slots):
        for n in range(nnz):
            entry = row * nnz + n
            code = codes[row, n]
            chosen = jnp.int32(slots)
            for slot in range(slots):
                chosen = jnp.where(code == 2 * slots + slot, keep[row][slot], chosen)
            kept.append(chosen)
            word = table[row * OFFSETS * slots + code]
            first = lax.shift_right_logical(word, 30)
            at = jnp.where(first == 1, near, slots * nnz - 1 - entry + near)
            todo[at] = (word & ((1 << 30) - 1)) + entry
            near = near + first
    todo[slots * nnz] = near

    for copy in large[:2]:
        copy.wait()
    width = out.shape[2]
    for row in range(slots):
        if row == 0:
            large[2].wait()
        total = None
        for n in range(nnz):
            term = jnp.dot(held[row, n], base[kept[row * nnz + n]], preferred_element_type=jnp.float32)
            total = term if total is None else total + term
        factor = jnp.broadcast_to(omega * scale[row : row + 1, :], (width, scale.shape[1])).T
        value = base[row].astype(jnp.float32) - factor * total
        value = jnp.where(row < live, value, 0.0).astype(out.dtype)
        out[row] = value
        flipped[row] = value.T


def prolong_call(counts, *arrays):
    neighbours, coarse_map, blocks, tentative, inv_diag = arrays
    slots, pores, width = tentative.shape
    nnz = neighbours.shape[1]
    arrays = [pltpu.with_memory_space_constraint(x, pltpu.HBM) for x in arrays]
    return pl.pallas_call(
        prolong_kernel,
        out_shape=(
            jax.ShapeDtypeStruct(tentative.shape, tentative.dtype),
            jax.ShapeDtypeStruct((slots, width, pores), tentative.dtype),
            jax.ShapeDtypeStruct((slots * nnz + 8,), jnp.int32),
        ),
        in_specs=[SMEM] + [ANY] * len(arrays),
        out_specs=(VMEM, VMEM, SMEM),
        scratch_shapes=[
            pltpu.VMEM(blocks.shape, blocks.dtype),
            pltpu.VMEM((slots + 1, pores, width), tentative.dtype),
            pltpu.VMEM(inv_diag.shape, inv_diag.dtype),
            pltpu.SMEM(neighbours.shape, jnp.int32),
            pltpu.SMEM(coarse_map.shape, jnp.int32),
            pltpu.SMEM((slots * OFFSETS * slots,), jnp.int32),
            pltpu.SemaphoreType.DMA((5,)),
        ],
        compiler_params=pltpu.CompilerParams(vmem_limit_bytes=16 << 20),
        cost_estimate=pl.CostEstimate(flops=100_000_000, bytes_accessed=1_000_000, transcendentals=0),
        name="prolong",
    )(counts, *arrays)


def galerkin_kernel(far, layout, parts, nnz, words, blocks, flipped, *refs):
    slots = flipped.shape[0]
    panels = FAR if far else NEAR
    dests = NCG * panels * NCG
    halo, refs = refs[:panels], refs[panels:]
    *refs, todo, sem = refs
    list_copy = pltpu.make_async_copy(words, todo, sem)
    list_copy.start()
    carried, refs = refs[: sum(carry for _, carry in layout)], refs[sum(carry for _, carry in layout) :]
    outs, (pool, acc) = refs[: len(layout)], refs[len(layout) :]
    for panel in range(panels):
        for slot in range(slots):
            pool[panel * slots + slot] = halo[panel][slot]
    acc[...] = jnp.zeros_like(acc)
    entries = slots * nnz
    list_copy.wait()
    near = todo[entries]
    count = entries - near if far else near

    batch = nnz

    def some(step, carry):
        grams, places = [], []
        for j in range(batch):
            at = step * batch + j
            word = todo[entries - 1 - at if far else at]
            dest = lax.shift_right_logical(word, 16)
            panel = lax.shift_right_logical(word, 8) & 255
            entry = word & 255
            inside = at < count
            places.append(jnp.where(inside, dest, dests))
            panel = jnp.where(inside, panel, 0)
            row = lax.div(entry, nnz)
            pair = jnp.dot(blocks[entry], pool[panel], preferred_element_type=jnp.float32).astype(pool.dtype)
            grams.append(jnp.dot(flipped[row], pair, preferred_element_type=jnp.float32))
        for place, gram in zip(places, grams):
            acc[place] = acc[place] + gram
        return carry

    if far:
        for step in range(entries // batch):
            some(step, 0)
    else:
        lax.fori_loop(0, lax.div(count + batch - 1, batch), some, 0)

    for (distance, carry), out in zip(layout, outs):
        rows = out.shape[1]
        start = 0
        if parts > 1:
            target = (lax.rem(lax.axis_index("grp") + distance, parts)) if far else (lax.axis_index("grp") ^ distance)
            start = pl.multiple_of(target * rows, rows)
        skip = out.shape[0] - dests
        if carry:
            source, carried = carried[0], carried[1:]
            out[pl.ds(0, skip)] = source[...]
        for dest in range(dests):
            out[skip + dest] = acc[dest, pl.ds(start, rows), :].astype(out.dtype)


def galerkin_call(far, layout, parts, todo, blocks, flipped, halo, carried):
    slots, width, pores = flipped.shape
    nnz = blocks.shape[1]
    panels = FAR if far else NEAR
    dests = NCG * panels * NCG
    rows = width // parts
    before = [carried[0].shape[0] if carry else 0 for _, carry in layout]
    return pl.pallas_call(
        functools.partial(galerkin_kernel, far, layout, parts, nnz),
        out_shape=[
            jax.ShapeDtypeStruct((skip + dests, rows, width), flipped.dtype if distance else jnp.float32)
            for (distance, _), skip in zip(layout, before)
        ],
        in_specs=[pl.BlockSpec(memory_space=pl.ANY), VMEM, VMEM] + [VMEM] * (len(halo) + len(carried)),
        out_specs=[VMEM] * len(layout),
        scratch_shapes=[
            pltpu.VMEM((panels * slots, pores, width), flipped.dtype),
            pltpu.VMEM((dests + 1, width, width), jnp.float32),
            pltpu.SMEM(todo.shape, jnp.int32),
            pltpu.SemaphoreType.DMA,
        ],
        compiler_params=pltpu.CompilerParams(vmem_limit_bytes=24 << 20),
        cost_estimate=pl.CostEstimate(flops=200_000_000, bytes_accessed=2_000_000, transcendentals=0),
        name="far" if far else "near",
    )(todo, blocks.reshape(slots * nnz, pores, pores), flipped, *halo, *carried)


def finish_kernel(nears, fars, boths, *refs):
    near, refs = refs[:nears], refs[nears:]
    far, refs = refs[:fars], refs[fars:]
    both, (out, held, sem) = refs[:boths], refs[boths:]
    odd = lax.rem(lax.axis_index("blk"), 2) == 1
    skip = NCG * NEAR * NCG
    for pieces, panels, first in ((near, NEAR, 0), (far, FAR, skip)):
        for c in range(NCG):
            for panel in range(panels):
                if panels == NEAR:
                    offset = jnp.where(odd, 1, 3) if panel else 2
                else:
                    offset = (0, 4, jnp.where(odd, 3, 1))[panel]
                base = (c * panels + panel) * NCG
                for c2 in range(NCG):
                    dest = base + c2
                    total = pieces[0][dest].astype(jnp.float32)
                    for piece in pieces[1:]:
                        total = total + piece[dest].astype(jnp.float32)
                    for piece in both:
                        total = total + piece[first + dest].astype(jnp.float32)
                    held[first + dest] = total
                pltpu.make_async_copy(held.at[pl.ds(first + base, NCG)], out.at[c, offset], sem).start()
    pltpu.make_async_copy(held, held, sem).wait()


def finish_call(near, far, both, rows, width):
    return pl.pallas_call(
        functools.partial(finish_kernel, len(near), len(far), len(both)),
        out_shape=jax.ShapeDtypeStruct((NCG, OFFSETS, NCG, rows, width), jnp.float32),
        in_specs=[VMEM] * (len(near) + len(far) + len(both)),
        out_specs=ANY,
        scratch_shapes=[
            pltpu.VMEM((NCG * OFFSETS * NCG, rows, width), jnp.float32),
            pltpu.SemaphoreType.DMA,
        ],
        compiler_params=pltpu.CompilerParams(vmem_limit_bytes=16 << 20),
        cost_estimate=pl.CostEstimate(flops=1_000_000, bytes_accessed=1_500_000, transcendentals=0),
        name="finish",
    )(*near, *far, *both)


def local(blocks, neighbours, tentative, inv_diag, coarse_map, counts):
    parts = lax.axis_size("grp")
    slots, pores, width = tentative.shape
    nnz = neighbours.shape[1]
    own, flipped, todo = prolong_call(
        counts, neighbours, jnp.transpose(coarse_map, (1, 2, 0)), blocks, tentative, inv_diag
    )
    sibling = from_sibling(own)
    behind = from_behind(own, "blk", 2)
    ahead = from_behind(own, "blk", -2)
    across = from_across(own)

    split = parts in ORDER
    share = parts if split else 1
    early = EARLY[parts] if split else []
    late = []
    layout = [(0, False)] + [(d, False) for d in early + late]
    near = galerkin_call(False, layout, share, todo, blocks, flipped, [own, sibling], [])
    near_own, near_early, near_late = near[0], near[1 : 1 + len(early)], near[1 + len(early) :]
    near_early = [from_partner(piece, d) for piece, d in zip(near_early, early)]
    layout = [(0, False)] + [(d, False) for d in early] + [(d, True) for d in late]
    far = galerkin_call(True, layout, share, todo, blocks, flipped, [behind, ahead, across], near_late)
    if near_early:
        far, at = list(far), 1 + early.index(ORDER[parts][-1])
        near_early, far[at] = lax.optimization_barrier((near_early, far[at]))
    far_own, far_early, both = far[0], far[1 : 1 + len(early)], far[1 + len(early) :]
    order = [d for d in ORDER[parts]] if split else []
    moved = {d: from_behind(piece, "grp", d) for d, piece in sorted(
        zip(early + late, far_early + both), key=lambda item: order.index(item[0]))}
    far_early = [moved[d] for d in early]
    both = [moved[d] for d in late]
    if not split:
        near_own, far_own = gathered(near_own, parts), gathered(far_own, parts)
    return finish_call(
        [near_own] + near_early, [far_own] + far_early, both, width // parts, width
    )


EARLY = {1: [], 2: [1], 4: [2, 3, 1]}
ORDER = {1: [], 2: [1], 4: [1, 2, 3]}


def gathered(whole, parts):
    dests, width, _ = whole.shape
    pieces = whole.astype(jnp.bfloat16).reshape(dests, parts, width // parts, width)
    arrived = lax.all_to_all(pieces, "grp", 1, 1, tiled=True)
    return jnp.sum(arrived.astype(jnp.float32), axis=1)


def solution(mesh):
    return jax.shard_map(
        local,
        mesh=mesh,
        in_specs=(
            P(("blk", "grp"), None, None, None),
            P(("blk", "grp"), None),
            P(("blk", "grp"), None, None),
            P(("blk", "grp"), None),
            P(None, "grp", None),
            P(("blk", "grp")),
        ),
        out_specs=P("blk", None, None, "grp", None),
        check_vma=False,
    )
```
